32 devices in a mesh: dp: 8 (over y, x, core), eshard: 4 (over z).
Axes of the slice: x: 2, y: 2, z: 4, core: 2. Of those that a mesh axis runs over, the one named last changes fastest.
Arguments:
- tokens: bfloat16 [2048, 4096], P('dp', 'eshard'), may hold values from -6 to 6
- cotangent: bfloat16 [2048, 4096], P('dp', 'eshard'), may hold values from -6 to 6
- route_ids: int32 [2048, 2], P('dp'), may hold values from 0 to 63, all different within a row; in each aligned block of 256 rows (0 to 255, 256 to 511, ...) at most 16 rows name the same one
- gate_fixed: int32 [2048, 2], P('dp'), may hold values from 1 to 65535
- w_gate: bfloat16 [4096, 32768], P('eshard', 'dp'), may hold values from -0.09375 to 0.09375
- w_up: bfloat16 [4096, 32768], P('eshard', 'dp'), may hold values from -0.09375 to 0.09375
- w_down: bfloat16 [32768, 4096], P('dp', 'eshard'), may hold values from -0.0625 to 0.0625
Outputs:
- mixed: bfloat16 [2048, 4096], P('dp', 'eshard')
- token_grad: bfloat16 [2048, 4096], P('dp', 'eshard')
- grad_w_gate: bfloat16 [4096, 32768], P('eshard', 'dp')
- grad_w_up: bfloat16 [4096, 32768], P('eshard', 'dp')
- grad_w_down: bfloat16 [32768, 4096], P('dp', 'eshard')
The draws below stay inside these ranges and needn't reach their ends.
Inputs may be any that keep to these rules, and one draw needn't show every extreme that they name: `route_ids`: the two ids of a token differ; among the 256 tokens of one index of dp, no id is named by more than 16 routes, a bound that some block reaches.
All inputs are finite; a program needn't handle non-finite values.
Results may differ from the reference program's by a relative error of at most 0.028.
Values may be sent and summed in bfloat16 or wider, within the bound.
A program may use at most 128 MiB of HBM per device.

```python
import math
import jax
import jax.numpy as jnp
import numpy as np
from jax import lax

D = 4096
HIDDEN_SIZE = 8192
ROUTED = 64
EXPERTS = 4
TOK_DEV = 256
CAP = 16
TOKENS = 2048
N_DP = 8
N_ESHARD = 4


def set_ends(drawn, rng, least, largest):
    longest = drawn.shape.index(max(drawn.shape))
    spots = []
    for shift in (0, 1):
        where = [jax.random.randint(jax.random.fold_in(rng, axis), (), 0, length) for axis, length in enumerate(drawn.shape)]
        where[longest] = (where[longest] + shift) % drawn.shape[longest]
        spots.append(tuple(where))
    return drawn.at[spots[0]].set(least).at[spots[1]].set(largest)


def block_levels(rng, dims, split, low, high):
    level = 1.0
    for position, parts in split:
        heights = jax.random.uniform(jax.random.fold_in(jax.random.fold_in(rng, 6), position), (parts,), jnp.float32, low / len(split), high / len(split))
        level = level * jnp.repeat(jnp.exp(heights), dims[position] // parts).reshape((-1,) + (1,) * (len(dims) - 1 - position))
    return level


def assign_block(rng, own, number, rows, number_of, top, reach, skew):
    ranking = jax.random.permutation(rng, number_of)
    packed, common = portions_of(number_of, rows * top, reach, skew, True), portions_of(number_of, rows * top, reach, skew, False)
    places = jnp.arange(number_of)

    def named(sizes, turn):
        used = int((sizes > 0).sum())
        fixed = max(1, used // 4)
        passed = fixed + (places - fixed + turn * (used - fixed)) % max(1, number_of - fixed)
        return jnp.zeros((number_of,), jnp.int32).at[ranking[jnp.where(places < fixed, places, passed)]].set(jnp.asarray(sizes, jnp.int32))

    sizes = jnp.where(number % 4 == 0, named(packed, number // 4), named(common, number - number // 4 - 1))
    mixed = jax.random.permutation(jax.random.fold_in(own, 3), number_of)
    giver, receiver = mixed[0:number_of // 2 * 2:2], mixed[1:number_of // 2 * 2:2]
    margin = jnp.minimum(sizes[giver] - 1, reach - sizes[receiver]) // 2
    margin = jnp.where((giver == ranking[0]) | (receiver == ranking[0]) | (sizes[receiver] == 0), 0, jnp.maximum(margin, 0))
    passed = jax.random.randint(jax.random.fold_in(own, 4), (number_of // 2,), 0, 1 << 20) % (margin + 1)
    sizes = sizes.at[giver].add(-passed).at[receiver].add(passed)
    labels = jnp.searchsorted(jnp.cumsum(sizes), jnp.arange(rows * top), side="right").astype(jnp.int32)
    table = labels.reshape(top, rows).T
    table = table[jax.random.permutation(jax.random.fold_in(own, 1), rows)]
    turn = jax.random.randint(jax.random.fold_in(own, 2), (rows, 1), 0, top)
    return jnp.take_along_axis(table, (jnp.arange(top)[None, :] + turn) % top, axis=1)


def portions_of(count, total, reach, slope, full):
    loads = [(1 << 20) // math.isqrt(grade ** slope) + 1 for grade in range(1, count + 1)]
    largest = reach if full else min(reach, max(-(-total // count), total * loads[0] // sum(loads)))
    least = 1 if total - largest >= count - 1 else 0
    given, rest = [largest] + [least] * (count - 1), total - largest - least * (count - 1)
    while rest > 0:
        movable = [i for i in range(1, count) if given[i] < largest] or [i for i in range(1, count) if given[i] < reach]
        pool, budget = sum([loads[i] for i in movable]), rest
        for i in movable:
            more = min(reach - given[i], max(1, budget * loads[i] // pool), rest)
            given[i] = given[i] + more
            rest = rest - more
    return np.array(given)


def scatter_about(rng, shape, deviation, bound, shards=(), held_as=jnp.bfloat16):
    drawn = deviation * jax.random.normal(rng, shape, jnp.float32)
    if shards:
        drawn = drawn * block_levels(rng, shape, shards, -0.22, 0.18)
    return jnp.clip(drawn, -bound, bound).astype(held_as)


def setup_inputs(seed: int = 0) -> dict:
    key_of = jax.random.split(jax.random.key(seed), 8)
    tokens = scatter_about(key_of[0], (TOKENS, D), 1.0, 6.0, ((0, 8), (1, 4)))
    cotangent = scatter_about(key_of[1], (TOKENS, D), 1.0, 6.0, ((0, 8), (1, 4)))
    route_ids_keys = jax.random.split(jax.random.fold_in(key_of[2], 1), TOKENS // TOK_DEV)
    route_ids_turns = jax.random.permutation(jax.random.fold_in(key_of[2], 3), TOKENS // TOK_DEV)
    route_ids = jax.vmap(lambda own, number: assign_block(jax.random.fold_in(key_of[2], 2), own, number, TOK_DEV, ROUTED, 2, CAP, 2))(route_ids_keys, route_ids_turns).reshape((TOKENS, 2))
    gate_fixed = set_ends(jax.random.randint(key_of[3], (TOKENS, 2), 1, 65536), jax.random.fold_in(key_of[3], 1), 1, 65535).astype(jnp.int32)
    w_gate = scatter_about(key_of[4], (D, EXPERTS * HIDDEN_SIZE), D ** -0.5, 0.09375, ((0, 4), (1, 8)))
    w_up = scatter_about(key_of[5], (D, EXPERTS * HIDDEN_SIZE), D ** -0.5, 0.09375, ((0, 4), (1, 8)))
    w_down = scatter_about(key_of[6], (EXPERTS * HIDDEN_SIZE, D), HIDDEN_SIZE ** -0.5, 0.0625, ((0, 8), (1, 4)))
    return {"tokens": tokens, "cotangent": cotangent, "route_ids": route_ids, "gate_fixed": gate_fixed, "w_gate": w_gate, "w_up": w_up, "w_down": w_down}


def routing(ids, gates):
    expert_ids = jnp.arange(EXPERTS, dtype=jnp.int32)
    hits = (ids[:, :, None] == expert_ids[None, None, :]).astype(jnp.int32)
    hit_tok = jnp.sum(hits, axis=1).astype(jnp.int32)
    gate_values = gates.astype(jnp.float32) / 65536.0
    weight_tok = jnp.sum(hits.astype(jnp.float32) * gate_values[:, :, None], axis=1)
    slots = (jnp.cumsum(hit_tok, axis=0) - hit_tok).astype(jnp.int32)
    target = expert_ids[None, :] * CAP + slots
    rows = jnp.arange(EXPERTS * CAP, dtype=jnp.int32)
    match = (target[None, :, :] == rows[:, None, None]).astype(jnp.float32) * hit_tok[None, :, :].astype(jnp.float32)
    select = jnp.sum(match, axis=2)
    weighted = jnp.sum(match * weight_tok[None, :, :], axis=2)
    return select, weighted


def block_sum(left, right, transpose_right):
    blocks = D // N_ESHARD
    total = None
    for piece in range(N_ESHARD):
        lhs = left[:, piece * blocks:(piece + 1) * blocks]
        if transpose_right:
            rhs = jnp.transpose(right[:, piece * blocks:(piece + 1) * blocks])
        else:
            rhs = right[piece * blocks:(piece + 1) * blocks, :]
        term = jnp.dot(lhs, rhs, preferred_element_type=jnp.float32).astype(jnp.bfloat16).astype(jnp.float32)
        total = term if total is None else total + term
    return total


def reference(tokens, cotangent, route_ids, gate_fixed, w_gate, w_up, w_down):
    ids = route_ids.reshape(N_DP, TOK_DEV, 2)
    gates = gate_fixed.reshape(N_DP, TOK_DEV, 2)
    select, weighted = jax.vmap(routing)(ids, gates)
    tok = tokens.reshape(N_DP, TOK_DEV, D).astype(jnp.float32)
    cot = cotangent.reshape(N_DP, TOK_DEV, D).astype(jnp.float32)
    hp = lax.Precision.HIGHEST
    x_rows = jnp.einsum('bit,btd->bid', select, tok, precision=hp).astype(jnp.bfloat16)
    g_rows = jnp.einsum('bit,btd->bid', weighted, cot, precision=hp).astype(jnp.bfloat16)
    x_rows = jnp.transpose(x_rows.reshape(N_DP, EXPERTS, CAP, D), (1, 0, 2, 3)).reshape(EXPERTS, N_DP * CAP, D)
    g_rows = jnp.transpose(g_rows.reshape(N_DP, EXPERTS, CAP, D), (1, 0, 2, 3)).reshape(EXPERTS, N_DP * CAP, D)
    outs_y = []
    outs_dx = []
    grads_gate = []
    grads_up = []
    grads_down = []
    for expert in range(EXPERTS):
        inputs = x_rows[expert]
        route_grad = g_rows[expert]
        wg = w_gate[:, expert * HIDDEN_SIZE:(expert + 1) * HIDDEN_SIZE]
        wu = w_up[:, expert * HIDDEN_SIZE:(expert + 1) * HIDDEN_SIZE]
        wd = w_down[expert * HIDDEN_SIZE:(expert + 1) * HIDDEN_SIZE, :]
        gate_pre = block_sum(inputs, wg, False)
        up_pre = block_sum(inputs, wu, False)
        logistic = jax.nn.sigmoid(gate_pre)
        activated = gate_pre * logistic
        hidden = (activated * up_pre).astype(jnp.bfloat16)
        outs_y.append(jnp.dot(hidden, wd, preferred_element_type=jnp.float32))
        grad_hidden = block_sum(route_grad, wd, True)
        gate_grad = (grad_hidden * up_pre * logistic * (1.0 + gate_pre * (1.0 - logistic))).astype(jnp.bfloat16)
        up_grad = (grad_hidden * activated).astype(jnp.bfloat16)
        grads_gate.append(jnp.dot(jnp.transpose(inputs), gate_grad, preferred_element_type=jnp.float32).astype(jnp.bfloat16))
        grads_up.append(jnp.dot(jnp.transpose(inputs), up_grad, preferred_element_type=jnp.float32).astype(jnp.bfloat16))
        grads_down.append(jnp.dot(jnp.transpose(hidden), route_grad, preferred_element_type=jnp.float32).astype(jnp.bfloat16))
        back = jnp.dot(gate_grad, jnp.transpose(wg), preferred_element_type=jnp.float32)
        back = back + jnp.dot(up_grad, jnp.transpose(wu), preferred_element_type=jnp.float32)
        outs_dx.append(back)
    expert_out = jnp.stack(outs_y).reshape(EXPERTS, N_DP, CAP, D)
    expert_out = jnp.transpose(expert_out, (1, 0, 2, 3)).reshape(N_DP, EXPERTS * CAP, D)
    back_rows = jnp.stack(outs_dx).reshape(EXPERTS, N_DP, CAP, D)
    back_rows = jnp.transpose(back_rows, (1, 0, 2, 3)).reshape(N_DP, EXPERTS * CAP, D)
    mixed = jnp.einsum('bit,bid->btd', weighted, expert_out, precision=hp).reshape(TOKENS, D).astype(jnp.bfloat16)
    token_grad = jnp.einsum('bit,bid->btd', select, back_rows, precision=hp).reshape(TOKENS, D).astype(jnp.bfloat16)
    grad_w_gate = jnp.concatenate(grads_gate, axis=1)
    grad_w_up = jnp.concatenate(grads_up, axis=1)
    grad_w_down = jnp.concatenate(grads_down, axis=0)
    return (mixed, token_grad, grad_w_gate, grad_w_up, grad_w_down)
```

```python
import functools

import jax
import jax.numpy as jnp
from jax import lax
from jax.experimental import pallas as pl
from jax.experimental.pallas import tpu as pltpu
from jax.sharding import PartitionSpec as P

EXPERTS = 4
CAP = 16
CORES = 2
WIDTH = 256
SPAN = 4
GRAD_WIDTH = 512
VMEM_BYTES = 48 * 1024 * 1024
GRAD_BYTES = 34 * 1024 * 1024


MESH = pl.DeviceIdType.MESH


def contract_cols(left, right):
    return lax.dot_general(
        left, right, (((1,), (1,)), ((), ())), preferred_element_type=jnp.float32
    )


def halves(value):
    high = value.astype(jnp.bfloat16)
    return high, (value - high.astype(jnp.float32)).astype(jnp.bfloat16)


def routing(ids, gates, cap):
    tokens = ids.shape[1]
    f32 = jnp.float32
    values = gates.astype(f32) * (1.0 / 65536.0)
    hits, weights = [], []
    for expert in range(EXPERTS):
        named = (ids == expert).astype(f32)
        hits.append(jnp.sum(named, axis=0, keepdims=True))
        weights.append(jnp.sum(named * values, axis=0, keepdims=True))
    hit = jnp.concatenate(hits, axis=0)
    earlier = (
        lax.broadcasted_iota(jnp.int32, (tokens, tokens), 0)
        < lax.broadcasted_iota(jnp.int32, (tokens, tokens), 1)
    ).astype(jnp.bfloat16)
    slots = jnp.dot(hit.astype(jnp.bfloat16), earlier, preferred_element_type=f32)
    places = lax.broadcasted_iota(jnp.int32, (cap, tokens), 0).astype(f32)
    select, weighted = [], []
    for expert in range(EXPERTS):
        here = (places == slots[expert : expert + 1]).astype(f32) * hits[expert]
        select.append(here)
        weighted.append(here * weights[expert])
    return jnp.concatenate(select, axis=0), jnp.concatenate(weighted, axis=0)


def window_kernel(
    size, groups, members, chunks, width, cap, span, first,
    ids_ref, gates_ref, tokens_ref, cot_ref, wg_ref, wu_ref, wd_ref,
    hid_ref, gg_ref, ug_ref, xt_ref, g_ref, back_ref, pick_ref,
    ids_v, gates_v, tokens_v, cot_v, tok_ref, grd_ref, wg_v, wu_v, wd_v, x_v, g_v,
    part_t, outer_t, inner_t, full_t, slope_t, silu_t,
    part_w, outer_w, inner_w, full_w, slope_w, silu_w,
    out_acc, back_acc, y_send, y_recv,
    a_sem, w_sem, xs_sem, xr_sem, in_sem, outer_sem, inner_sem, out_sem, ys_sem, yr_sem,
):
    f32, bf16 = jnp.float32, jnp.bfloat16
    me, z = lax.axis_index("dp"), lax.axis_index("eshard")
    chips = groups // CORES
    chip, core = me // CORES, lax.rem(me, CORES)
    feats = tok_ref.shape[1]
    near = CORES * cap
    rows = groups * cap
    wides = chunks // span
    units = chunks + wides
    half = size // 2
    left = z < half
    middle = jnp.logical_or(z == half - 1, z == half)
    tip = jnp.logical_or(z == 0, z == size - 1)
    inward = jnp.where(left, z + 1, z - 1)
    outward = jnp.where(tip, z, jnp.where(left, z - 1, z + 1))
    distance = jnp.where(left, half - 1 - z, z - half)

    small = tuple(
        pltpu.make_async_copy(src, dst, a_sem.at[i])
        for i, (src, dst) in enumerate(
            ((ids_ref, ids_v), (gates_ref, gates_v), (tokens_ref, tokens_v), (cot_ref, cot_v))
        )
    )
    for copy in small:
        copy.start()

    def weight_copy(c, k):
        cols = pl.ds(pl.multiple_of(c * width, width), width)
        if k == 0:
            return pltpu.make_async_copy(wg_ref.at[:, cols], wg_v.at[c], w_sem.at[c, 0])
        if k == 1:
            return pltpu.make_async_copy(wu_ref.at[:, cols], wu_v.at[c], w_sem.at[c, 1])
        return pltpu.make_async_copy(wd_ref.at[cols, :], wd_v.at[c], w_sem.at[c, 2])

    for k in range(3):
        for c in range(span):
            weight_copy(c, k).start()

    barrier = pltpu.get_barrier_semaphore()

    @pl.loop(1, groups)
    def _(k):
        pl.semaphore_signal(
            barrier, inc=1, device_id={"dp": lax.rem(me + k, groups)}, device_id_type=MESH
        )

    pl.semaphore_signal(barrier, inc=1, device_id={"eshard": inward}, device_id_type=MESH)

    @pl.when(jnp.logical_not(tip))
    def _():
        pl.semaphore_signal(barrier, inc=1, device_id={"eshard": outward}, device_id_type=MESH)

    small[0].wait()
    small[1].wait()
    select, weighted = routing(ids_v[...], gates_v[...], cap)
    small[2].wait()
    tok_ref[...] = jnp.dot(
        select.astype(bf16), tokens_v[...], preferred_element_type=f32
    ).astype(bf16)

    pl.semaphore_wait(barrier, groups + jnp.where(tip, 0, 1))

    def device_of(slot):
        return lax.rem(chip + slot // CORES, chips) * CORES + lax.rem(slot, CORES)

    def row_copy(src, dst, which, slot):
        to = device_of(slot)
        there = lax.rem(chips - slot // CORES, chips) * CORES + core
        return pltpu.make_async_remote_copy(
            src_ref=src.at[pl.ds(pl.multiple_of((to // members) * cap, cap), cap), :],
            dst_ref=dst.at[pl.ds(pl.multiple_of(there * cap, cap), cap), :],
            send_sem=xs_sem.at[which, slot],
            recv_sem=xr_sem.at[which, there],
            device_id={"dp": to},
            device_id_type=MESH,
        )

    def row_take(src, dst, which, slot):
        pltpu.make_async_remote_copy(
            src_ref=src.at[pl.ds(0, cap), :],
            dst_ref=dst.at[pl.ds(pl.multiple_of(slot * cap, cap), cap), :],
            send_sem=xs_sem.at[which, slot],
            recv_sem=xr_sem.at[which, slot],
            device_id={"dp": device_of(slot)},
            device_id_type=MESH,
        ).wait_recv()

    def send_near(which, src, dst):
        row_copy(src, dst, which, 1 - core).start()
        own = pl.multiple_of((me // members) * cap, cap)
        dst[pl.ds(pl.multiple_of(core * cap, cap), cap), :] = src[pl.ds(own, cap), :]

    def send_far(which, src, dst):
        @pl.loop(CORES, groups)
        def _(slot):
            row_copy(src, dst, which, slot).start()

    def take_far(which, src, dst):
        @pl.loop(CORES, groups)
        def _(slot):
            row_take(src, dst, which, slot)

    send_near(0, tok_ref, x_v)
    high, low = halves(weighted)
    small[3].wait()
    grd_ref[...] = (
        jnp.dot(high, cot_v[...], preferred_element_type=f32)
        + jnp.dot(low, cot_v[...], preferred_element_type=f32)
    ).astype(bf16)
    send_near(1, grd_ref, g_v)
    send_far(0, tok_ref, x_v)
    send_far(1, grd_ref, g_v)

    @pl.loop(span, chunks)
    def _(c):
        for k in range(3):
            weight_copy(c, k).start()

    pick_ref[0] = jnp.transpose(select).astype(bf16)
    high, low = halves(jnp.transpose(weighted))
    pick_ref[1] = high
    pick_ref[2] = low
    out_acc[...] = jnp.zeros_like(out_acc)
    back_acc[...] = jnp.zeros_like(back_acc)

    class Kind:
        def __init__(self, part, outer, inner, full, slope, silu, r0, r1, parts):
            self.part, self.outer, self.inner, self.full = part, outer, inner, full
            self.slope, self.silu = slope, silu
            self.r0, self.r1, self.parts = r0, r1, parts

        def send(self, src, dst, i, t, k, sent, got, to):
            return pltpu.make_async_remote_copy(
                src_ref=src.at[i, k], dst_ref=dst.at[i, k],
                send_sem=sent.at[t, k], recv_sem=got.at[t, k],
                device_id={"eshard": to}, device_id_type=MESH,
            )

        def to_outer(self, i, t, k):
            return self.send(self.part, self.outer, i, t, k, in_sem, outer_sem, inward)

        def to_partner(self, i, t, k):
            return self.send(self.part, self.inner, i, t, k, in_sem, inner_sem, inward)

        def sum_out(self, i, t, k):
            return self.send(self.full, self.inner, i, t, k, out_sem, inner_sem, outward)

        def pass_out(self, i, t, k):
            return self.send(self.inner, self.inner, i, t, k, out_sem, inner_sem, outward)

        def columns(self, j):
            return pl.ds(j * width, width)

        def forward(self, i, t, k):
            self.to_partner(i, t, k).wait_recv()
            self.full[i, k] = (
                self.part[i, k].astype(f32) + self.inner[i, k].astype(f32)
            ).astype(bf16)

            @pl.when(jnp.logical_not(tip))
            def _():
                self.sum_out(i, t, k).start()

        def gather(self, i, t, k):
            own = []
            for j in range(self.parts):
                c = i * self.parts + j
                if k == 0:
                    value = jnp.dot(x_v[self.r0 : self.r1, :], wg_v[c], preferred_element_type=f32)
                elif k == 1:
                    value = jnp.dot(x_v[self.r0 : self.r1, :], wu_v[c], preferred_element_type=f32)
                else:
                    value = contract_cols(g_v[self.r0 : self.r1, :], wd_v[c])
                own.append(value)

            @pl.when(tip)
            def _():
                for j, value in enumerate(own):
                    self.part[i, k, :, self.columns(j)] = value.astype(bf16)

            @pl.when(jnp.logical_not(tip))
            def _():
                self.to_outer(i, t, k).wait_recv()
                for j, value in enumerate(own):
                    self.part[i, k, :, self.columns(j)] = (
                        value + self.outer[i, k, :, self.columns(j)].astype(f32)
                    ).astype(bf16)

            @pl.when(middle)
            def _():
                self.to_partner(i, t, k).start()

            @pl.when(jnp.logical_not(middle))
            def _():
                self.to_outer(i, t, k).start()

        def arrive(self, i, t, k):
            @pl.when(jnp.logical_not(middle))
            def _():
                self.to_partner(i, t, k).wait_recv()

            @pl.when(jnp.logical_not(jnp.logical_or(middle, tip)))
            def _():
                self.pass_out(i, t, k).start()

        def total(self, i, k, j):
            mine = self.part[i, k, :, self.columns(j)].astype(f32)
            return self.inner[i, k, :, self.columns(j)].astype(f32) + jnp.where(
                middle, mine, jnp.zeros_like(mine)
            )

        def activate(self, i, t):
            self.arrive(i, t, 0)
            self.arrive(i, t, 1)
            added = None
            for j in range(self.parts):
                c = i * self.parts + j
                gate, up = self.total(i, 0, j), self.total(i, 1, j)
                logistic = 1.0 / (1.0 + jnp.exp(-gate))
                silu = gate * logistic
                product = silu * up
                self.slope[:, self.columns(j)] = up * logistic * (1.0 + gate * (1.0 - logistic))
                self.silu[:, self.columns(j)] = silu
                term = jnp.dot(product.astype(bf16), wd_v[c], preferred_element_type=f32)
                added = term if added is None else added + term
                cols = pl.ds(pl.multiple_of(c * width, width), width)
                if self.r0:
                    product = jnp.concatenate(
                        (jnp.zeros((self.r0, width), f32), product), axis=0
                    )
                hid_ref[cols, self.r0 : self.r1] = jnp.transpose(product)[:, self.r0 :].astype(bf16)
            out_acc[self.r0 : self.r1, :] += added

        def differentiate(self, i, t):
            self.arrive(i, t, 2)
            added = None
            for j in range(self.parts):
                c = i * self.parts + j
                down = self.total(i, 2, j)
                gate_grad = (down * self.slope[:, self.columns(j)]).astype(bf16)
                up_grad = (down * self.silu[:, self.columns(j)]).astype(bf16)
                term = contract_cols(gate_grad, wg_v[c]) + contract_cols(up_grad, wu_v[c])
                added = term if added is None else added + term
                cols = pl.ds(pl.multiple_of(c * width, width), width)
                gg_ref[self.r0 : self.r1, cols] = gate_grad
                ug_ref[self.r0 : self.r1, cols] = up_grad
            back_acc[self.r0 : self.r1, :] += added

        def drain(self, i, t):
            for k in range(3):
                self.to_outer(i, t, k).wait_send()

                @pl.when(jnp.logical_not(tip))
                def _():
                    self.sum_out(i, t, k).wait_send()

    tall = Kind(part_t, outer_t, inner_t, full_t, slope_t, silu_t, near, rows, 1)
    wide = Kind(part_w, outer_w, inner_w, full_w, slope_w, silu_w, 0, near, span)

    def return_copy(which, slot):
        to = device_of(slot)
        return pltpu.make_async_remote_copy(
            src_ref=y_send.at[which, slot], dst_ref=y_recv.at[which, me],
            send_sem=ys_sem.at[which, slot],
            recv_sem=yr_sem.at[which, me],
            device_id={"dp": to}, device_id_type=MESH,
        )

    def return_take(which, slot):
        source = device_of(slot)
        pltpu.make_async_remote_copy(
            src_ref=y_send.at[which, slot], dst_ref=y_recv.at[which, source],
            send_sem=ys_sem.at[which, slot],
            recv_sem=yr_sem.at[which, source],
            device_id={"dp": source}, device_id_type=MESH,
        ).wait()

    def home_far(which, acc):
        y_send[which, CORES:] = acc[near:, :].astype(bf16).reshape(groups - CORES, cap, feats)

        @pl.loop(CORES, groups)
        def _(slot):
            return_copy(which, slot).start()

    def home_near(which, acc):
        y_send[which, :CORES] = acc[:near, :].astype(bf16).reshape(CORES, cap, feats)
        return_copy(which, 1 - core).start()
        y_recv[which, me] = y_send[which, core]

    lag = jnp.where(middle, 2, 2 + 4 * distance)
    late = first + chunks

    def is_wide(t):
        return jnp.logical_and(
            jnp.logical_and(t >= 0, t < units), jnp.logical_or(t < first, t >= late)
        )

    def is_tall(t):
        return jnp.logical_and(t >= first, t < late)

    def wide_index(t):
        return jnp.where(t < first, t, t - chunks)

    def wait_weights(i, parts, k):
        for j in range(parts):
            weight_copy(i * parts + j, k).wait()

    @pl.loop(0, units + 2 + 4 * (half - 1))
    def _(t):
        before, done = t - 1, t - lag
        for k in range(3):

            @pl.when(is_wide(t))
            def _():
                i = wide_index(t)

                @pl.when(t < first)
                def _():
                    wait_weights(i, span, k)

                if k != 1:

                    @pl.when(t == 0)
                    def _():
                        if k == 0:
                            row_take(tok_ref, x_v, 0, 1 - core)
                        else:
                            row_take(grd_ref, g_v, 1, 1 - core)

                wide.gather(i, t, k)

            @pl.when(is_tall(t))
            def _():
                i = t - first

                @pl.when(i >= first * span)
                def _():
                    wait_weights(i, 1, k)

                if k != 1:

                    @pl.when(i == 0)
                    def _():
                        if k == 0:
                            take_far(0, tok_ref, x_v)
                        else:
                            take_far(1, grd_ref, g_v)

                tall.gather(i, t, k)

            @pl.when(middle)
            def _():
                @pl.when(is_wide(before))
                def _():
                    wide.forward(wide_index(before), before, k)

                @pl.when(is_tall(before))
                def _():
                    tall.forward(before - first, before, k)

            if k == 0:

                @pl.when(is_wide(done))
                def _():
                    wide.activate(wide_index(done), done)

                @pl.when(is_tall(done))
                def _():
                    tall.activate(done - first, done)

                @pl.when(done == late - 1)
                def _():
                    home_far(0, out_acc)

                @pl.when(done == units - 1)
                def _():
                    home_near(0, out_acc)

            if k == 1:

                @pl.when(is_wide(done))
                def _():
                    wide.differentiate(wide_index(done), done)

                @pl.when(is_tall(done))
                def _():
                    tall.differentiate(done - first, done)

                @pl.when(done == late - 1)
                def _():
                    home_far(1, back_acc)

                @pl.when(done == units - 1)
                def _():
                    home_near(1, back_acc)

        @pl.when(t == first + 1)
        def _():
            xt_ref[...] = jnp.transpose(x_v[...].astype(f32)).astype(bf16)
            g_ref[...] = g_v[...]

    @pl.loop(0, units)
    def _(t):
        @pl.when(is_wide(t))
        def _():
            wide.drain(wide_index(t), t)

        @pl.when(is_tall(t))
        def _():
            tall.drain(t - first, t)

    for which in range(2):
        row_copy(tok_ref, x_v, which, 1 - core).wait_send()
        return_take(which, 1 - core)

        @pl.loop(CORES, groups)
        def _(slot):
            row_copy(tok_ref, x_v, which, slot).wait_send()
            return_take(which, slot)

    back_ref[...] = y_recv[...]


def run_window(ids, gates, tokens, cotangent, w_gate, w_up, w_down):
    groups, size = lax.axis_size("dp"), lax.axis_size("eshard")
    members = groups // EXPERTS
    feats, hidden = w_gate.shape
    cap, count = CAP, tokens.shape[0]
    rows, near = groups * cap, CORES * cap
    width = min(WIDTH, hidden)
    chunks = hidden // width
    span = SPAN if chunks % (2 * SPAN) == 0 else 1
    wides = chunks // span
    first = wides // 2
    units = chunks + wides
    bf16, f32 = jnp.bfloat16, jnp.float32
    vmem, hbm = pl.BlockSpec(memory_space=pltpu.VMEM), pl.BlockSpec(memory_space=pl.ANY)
    dma = pltpu.SemaphoreType.DMA
    gathered = jax.ShapeDtypeStruct((rows, hidden), bf16)
    tall = pltpu.VMEM((chunks, 3, rows - near, width), bf16)
    wide = pltpu.VMEM((wides, 3, near, span * width), bf16)
    tall_f32 = pltpu.VMEM((rows - near, width), f32)
    wide_f32 = pltpu.VMEM((near, span * width), f32)
    return pl.pallas_call(
        functools.partial(window_kernel, size, groups, members, chunks, width, cap, span, first),
        out_shape=(
            jax.ShapeDtypeStruct((hidden, rows), bf16), gathered, gathered,
            jax.ShapeDtypeStruct((feats, rows), bf16),
            jax.ShapeDtypeStruct((rows, feats), bf16),
            jax.ShapeDtypeStruct((2, groups, cap, feats), bf16),
            jax.ShapeDtypeStruct((3, count, EXPERTS * cap), bf16),
        ),
        in_specs=[hbm] * 7,
        out_specs=(vmem,) * 7,
        scratch_shapes=[
            pltpu.VMEM(ids.shape, jnp.int32),
            pltpu.VMEM(gates.shape, jnp.int32),
            pltpu.VMEM(tokens.shape, bf16),
            pltpu.VMEM(cotangent.shape, bf16),
            pltpu.VMEM((EXPERTS * cap, feats), bf16),
            pltpu.VMEM((EXPERTS * cap, feats), bf16),
            pltpu.VMEM((chunks, feats, width), bf16),
            pltpu.VMEM((chunks, feats, width), bf16),
            pltpu.VMEM((chunks, width, feats), bf16),
            pltpu.VMEM((rows, feats), bf16),
            pltpu.VMEM((rows, feats), bf16),
            tall, tall, tall, tall, tall_f32, tall_f32,
            wide, wide, wide, wide, wide_f32, wide_f32,
            pltpu.VMEM((rows, feats), f32),
            pltpu.VMEM((rows, feats), f32),
            pltpu.VMEM((2, groups, cap, feats), bf16),
            pltpu.VMEM((2, groups, cap, feats), bf16),
            dma((4,)), dma((chunks, 3)),
            dma((2, groups)), dma((2, groups)),
            dma((units, 3)), dma((units, 3)), dma((units, 3)), dma((units, 3)),
            dma((2, groups)), dma((2, groups)),
        ],
        compiler_params=pltpu.CompilerParams(
            collective_id=0, has_side_effects=True, vmem_limit_bytes=VMEM_BYTES
        ),
    )(ids, gates, tokens, cotangent, w_gate, w_up, w_down)


def gradient_kernel(
    members, width, xt_ref, gg_ref, ug_ref, hid_ref, g_ref, back_ref, pick_ref,
    mixed_ref, token_ref, gate_ref, up_ref, down_ref,
    mixed_v, token_v, gate_v, up_v, down_v, row_sem, sem,
):
    f32, bf16 = jnp.float32, jnp.bfloat16

    def product(left, right):
        return jnp.dot(left, right, preferred_element_type=f32)

    def copies(i):
        cols = pl.ds(pl.multiple_of(i * width, width), width)
        return (
            pltpu.make_async_copy(gate_v.at[i], gate_ref.at[:, cols], sem.at[i, 0]),
            pltpu.make_async_copy(up_v.at[i], up_ref.at[:, cols], sem.at[i, 1]),
            pltpu.make_async_copy(down_v.at[i], down_ref.at[cols, :], sem.at[i, 2]),
        )

    blocks = gate_v.shape[0]

    @pl.loop(0, blocks)
    def _(i):
        cols = pl.ds(pl.multiple_of(i * width, width), width)
        gate_copy, up_copy, down_copy = copies(i)
        gate_v[i] = product(xt_ref[...], gg_ref[:, cols]).astype(bf16)
        gate_copy.start()
        up_v[i] = product(xt_ref[...], ug_ref[:, cols]).astype(bf16)
        up_copy.start()
        down_v[i] = product(hid_ref[cols, :], g_ref[...]).astype(bf16)
        down_copy.start()

    def gathered(which):
        parts = []
        for expert in range(EXPERTS):
            total = back_ref[which, expert * members].astype(f32)
            for member in range(1, members):
                total = total + back_ref[which, expert * members + member].astype(f32)
            parts.append(total)
        return halves(jnp.concatenate(parts, axis=0))

    high, low = gathered(0)
    mixed_v[...] = (
        product(pick_ref[1], high) + product(pick_ref[2], high) + product(pick_ref[1], low)
    ).astype(bf16)
    mixed_copy = pltpu.make_async_copy(mixed_v, mixed_ref, row_sem.at[0])
    mixed_copy.start()
    high, low = gathered(1)
    token_v[...] = (product(pick_ref[0], high) + product(pick_ref[0], low)).astype(bf16)
    token_copy = pltpu.make_async_copy(token_v, token_ref, row_sem.at[1])
    token_copy.start()

    @pl.loop(0, blocks)
    def _(i):
        for copy in copies(i):
            copy.wait()

    mixed_copy.wait()
    token_copy.wait()


def run_gradients(count, hidden_t, gate_grad, up_grad, inputs_t, route_grad, back, pick):
    groups = lax.axis_size("dp")
    feats = inputs_t.shape[0]
    hidden = hidden_t.shape[0]
    width = min(GRAD_WIDTH, hidden)
    blocks = hidden // width
    bf16 = jnp.bfloat16
    vmem, hbm = pl.BlockSpec(memory_space=pltpu.VMEM), pl.BlockSpec(memory_space=pl.ANY)
    return pl.pallas_call(
        functools.partial(gradient_kernel, groups // EXPERTS, width),
        out_shape=(
            jax.ShapeDtypeStruct((count, feats), bf16),
            jax.ShapeDtypeStruct((count, feats), bf16),
            jax.ShapeDtypeStruct((feats, hidden), bf16),
            jax.ShapeDtypeStruct((feats, hidden), bf16),
            jax.ShapeDtypeStruct((hidden, feats), bf16),
        ),
        in_specs=[vmem] * 7,
        out_specs=(hbm,) * 5,
        scratch_shapes=[
            pltpu.VMEM((count, feats), bf16),
            pltpu.VMEM((count, feats), bf16),
            pltpu.VMEM((blocks, feats, width), bf16),
            pltpu.VMEM((blocks, feats, width), bf16),
            pltpu.VMEM((blocks, width, feats), bf16),
            pltpu.SemaphoreType.DMA((2,)),
            pltpu.SemaphoreType.DMA((blocks, 3)),
        ],
        compiler_params=pltpu.CompilerParams(vmem_limit_bytes=GRAD_BYTES),
    )(inputs_t, gate_grad, up_grad, hidden_t, route_grad, back, pick)


def on_device(tokens, cotangent, route_ids, gate_fixed, w_gate, w_up, w_down):
    hidden_t, gate_grad, up_grad, inputs_t, route_grad, back, pick = run_window(
        *(pltpu.with_memory_space_constraint(a, pltpu.HBM) for a in (jnp.transpose(route_ids), jnp.transpose(gate_fixed), tokens, cotangent)), w_gate, w_up, w_down
    )
    return run_gradients(
        tokens.shape[0], hidden_t, gate_grad, up_grad, inputs_t, route_grad, back, pick
    )


def solution(mesh):
    placed = (
        P("dp", "eshard"),
        P("dp", "eshard"),
        P("dp", None),
        P("dp", None),
        P("eshard", "dp"),
        P("eshard", "dp"),
        P("dp", "eshard"),
    )
    return jax.shard_map(
        on_device,
        mesh=mesh,
        in_specs=placed,
        out_specs=(
            P("dp", "eshard"),
            P("dp", "eshard"),
            P("eshard", "dp"),
            P("eshard", "dp"),
            P("dp", "eshard"),
        ),
        check_vma=False,
    )
```

```python
import functools

import jax
import jax.numpy as jnp
from jax import lax
from jax.experimental import pallas as pl
from jax.experimental.pallas import tpu as pltpu
from jax.sharding import PartitionSpec as P

EXPERTS = 4
CAP = 16
CORES = 2
WIDTH = 256
SPAN = 4
GRAD_WIDTH = 512
EARLY = 4
VMEM_BYTES = 43 * 1024 * 1024
GRAD_BYTES = 27 * 1024 * 1024


MESH = pl.DeviceIdType.MESH


def contract_cols(left, right):
    return lax.dot_general(
        left, right, (((1,), (1,)), ((), ())), preferred_element_type=jnp.float32
    )


def halves(value):
    high = value.astype(jnp.bfloat16)
    return high, (value - high.astype(jnp.float32)).astype(jnp.bfloat16)


def routing(ids, gates, cap):
    tokens = ids.shape[1]
    f32 = jnp.float32
    values = gates.astype(f32) * (1.0 / 65536.0)
    hits, weights = [], []
    for expert in range(EXPERTS):
        named = (ids == expert).astype(f32)
        hits.append(jnp.sum(named, axis=0, keepdims=True))
        weights.append(jnp.sum(named * values, axis=0, keepdims=True))
    hit = jnp.concatenate(hits, axis=0)
    earlier = (
        lax.broadcasted_iota(jnp.int32, (tokens, tokens), 0)
        < lax.broadcasted_iota(jnp.int32, (tokens, tokens), 1)
    ).astype(jnp.bfloat16)
    slots = jnp.dot(hit.astype(jnp.bfloat16), earlier, preferred_element_type=f32)
    places = lax.broadcasted_iota(jnp.int32, (cap, tokens), 0).astype(f32)
    select, weighted = [], []
    for expert in range(EXPERTS):
        here = (places == slots[expert : expert + 1]).astype(f32) * hits[expert]
        select.append(here)
        weighted.append(here * weights[expert])
    return jnp.concatenate(select, axis=0), jnp.concatenate(weighted, axis=0)


def window_kernel(
    size, groups, members, chunks, width, cap, span, early, broad,
    ids_ref, gates_ref, tokens_ref, cot_ref, wg_ref, wu_ref, wd_ref,
    hid_ref, gg_ref, ug_ref, xt_ref, g_ref, back_ref, pick_ref, soon_ref,
    ids_v, gates_v, tokens_v, cot_v, tok_ref, grd_ref, wg_v, wu_v, wd_v, x_v, g_v,
    part_t, outer_t, inner_t, full_t, slope_t, silu_t,
    part_w, outer_w, inner_w, full_w, slope_w, silu_w,
    part_f, outer_f, inner_f, full_f, slope_f, silu_f,
    out_acc, back_acc, y_send, y_recv,
    a_sem, w_sem, xs_sem, xr_sem, in_sem, outer_sem, inner_sem, out_sem, ys_sem, yr_sem,
):
    f32, bf16 = jnp.float32, jnp.bfloat16
    me, z = lax.axis_index("dp"), lax.axis_index("eshard")
    chips = groups // CORES
    chip, core = me // CORES, lax.rem(me, CORES)
    feats = tok_ref.shape[1]
    near = CORES * cap
    rows = groups * cap
    units = chunks + 2
    half = size // 2
    left = z < half
    middle = jnp.logical_or(z == half - 1, z == half)
    tip = jnp.logical_or(z == 0, z == size - 1)
    inward = jnp.where(left, z + 1, z - 1)
    outward = jnp.where(tip, z, jnp.where(left, z - 1, z + 1))
    distance = jnp.where(left, half - 1 - z, z - half)

    small = tuple(
        pltpu.make_async_copy(src, dst, a_sem.at[i])
        for i, (src, dst) in enumerate(
            ((ids_ref, ids_v), (gates_ref, gates_v), (tokens_ref, tokens_v), (cot_ref, cot_v))
        )
    )
    for copy in small:
        copy.start()

    def weight_copy(c, k):
        cols = pl.ds(pl.multiple_of(c * width, width), width)
        if k == 0:
            return pltpu.make_async_copy(wg_ref.at[:, cols], wg_v.at[c], w_sem.at[c, 0])
        if k == 1:
            return pltpu.make_async_copy(wu_ref.at[:, cols], wu_v.at[c], w_sem.at[c, 1])
        return pltpu.make_async_copy(wd_ref.at[cols, :], wd_v.at[c], w_sem.at[c, 2])

    for k in range(3):
        for c in range(span):
            weight_copy(c, k).start()

    barrier = pltpu.get_barrier_semaphore()

    @pl.loop(1, groups)
    def _(k):
        pl.semaphore_signal(
            barrier, inc=1, device_id={"dp": lax.rem(me + k, groups)}, device_id_type=MESH
        )

    pl.semaphore_signal(barrier, inc=1, device_id={"eshard": inward}, device_id_type=MESH)

    @pl.when(jnp.logical_not(tip))
    def _():
        pl.semaphore_signal(barrier, inc=1, device_id={"eshard": outward}, device_id_type=MESH)

    small[0].wait()
    small[1].wait()
    select, weighted = routing(ids_v[...], gates_v[...], cap)
    small[2].wait()
    tok_ref[...] = jnp.dot(
        select.astype(bf16), tokens_v[...], preferred_element_type=f32
    ).astype(bf16)

    pl.semaphore_wait(barrier, groups + jnp.where(tip, 0, 1))

    def device_of(slot):
        return lax.rem(chip + slot // CORES, chips) * CORES + lax.rem(slot, CORES)

    def row_copy(src, dst, which, slot):
        to = device_of(slot)
        there = lax.rem(chips - slot // CORES, chips) * CORES + core
        return pltpu.make_async_remote_copy(
            src_ref=src.at[pl.ds(pl.multiple_of((to // members) * cap, cap), cap), :],
            dst_ref=dst.at[pl.ds(pl.multiple_of(there * cap, cap), cap), :],
            send_sem=xs_sem.at[which, slot],
            recv_sem=xr_sem.at[which, there],
            device_id={"dp": to},
            device_id_type=MESH,
        )

    def row_take(src, dst, which, slot):
        pltpu.make_async_remote_copy(
            src_ref=src.at[pl.ds(0, cap), :],
            dst_ref=dst.at[pl.ds(pl.multiple_of(slot * cap, cap), cap), :],
            send_sem=xs_sem.at[which, slot],
            recv_sem=xr_sem.at[which, slot],
            device_id={"dp": device_of(slot)},
            device_id_type=MESH,
        ).wait_recv()

    def send_near(which, src, dst):
        row_copy(src, dst, which, 1 - core).start()
        own = pl.multiple_of((me // members) * cap, cap)
        dst[pl.ds(pl.multiple_of(core * cap, cap), cap), :] = src[pl.ds(own, cap), :]

    def send_far(which, src, dst):
        @pl.loop(CORES, groups)
        def _(slot):
            row_copy(src, dst, which, slot).start()

    def take_far(which, src, dst):
        @pl.loop(CORES, groups)
        def _(slot):
            row_take(src, dst, which, slot)

    send_near(0, tok_ref, x_v)
    high, low = halves(weighted)
    small[3].wait()
    grd_ref[...] = (
        jnp.dot(high, cot_v[...], preferred_element_type=f32)
        + jnp.dot(low, cot_v[...], preferred_element_type=f32)
    ).astype(bf16)
    send_near(1, grd_ref, g_v)
    send_far(0, tok_ref, x_v)
    send_far(1, grd_ref, g_v)

    @pl.loop(span, chunks)
    def _(c):
        for k in range(3):
            weight_copy(c, k).start()

    pick_ref[0] = jnp.transpose(select).astype(bf16)
    high, low = halves(jnp.transpose(weighted))
    pick_ref[1] = high
    pick_ref[2] = low
    out_acc[...] = jnp.zeros_like(out_acc)
    back_acc[...] = jnp.zeros_like(back_acc)

    class Kind:
        def __init__(self, part, outer, inner, full, slope, silu, r0, r1, parts):
            self.part, self.outer, self.inner, self.full = part, outer, inner, full
            self.slope, self.silu = slope, silu
            self.r0, self.r1, self.parts = r0, r1, parts

        def send(self, src, dst, i, t, k, sent, got, to):
            return pltpu.make_async_remote_copy(
                src_ref=src.at[i, k], dst_ref=dst.at[i, k],
                send_sem=sent.at[t, k], recv_sem=got.at[t, k],
                device_id={"eshard": to}, device_id_type=MESH,
            )

        def to_outer(self, i, t, k):
            return self.send(self.part, self.outer, i, t, k, in_sem, outer_sem, inward)

        def to_partner(self, i, t, k):
            return self.send(self.part, self.inner, i, t, k, in_sem, inner_sem, inward)

        def sum_out(self, i, t, k):
            return self.send(self.full, self.inner, i, t, k, out_sem, inner_sem, outward)

        def pass_out(self, i, t, k):
            return self.send(self.inner, self.inner, i, t, k, out_sem, inner_sem, outward)

        def columns(self, j):
            return pl.ds(j * width, width)

        def forward(self, i, t, k):
            self.to_partner(i, t, k).wait_recv()
            self.full[i, k] = (
                self.part[i, k].astype(f32) + self.inner[i, k].astype(f32)
            ).astype(bf16)

            @pl.when(jnp.logical_not(tip))
            def _():
                self.sum_out(i, t, k).start()

        def gather(self, i, c0, t, k):
            own = []
            for j in range(self.parts):
                c = c0 + j
                if k == 0:
                    value = jnp.dot(x_v[self.r0 : self.r1, :], wg_v[c], preferred_element_type=f32)
                elif k == 1:
                    value = jnp.dot(x_v[self.r0 : self.r1, :], wu_v[c], preferred_element_type=f32)
                else:
                    value = contract_cols(g_v[self.r0 : self.r1, :], wd_v[c])
                own.append(value)

            @pl.when(tip)
            def _():
                for j, value in enumerate(own):
                    self.part[i, k, :, self.columns(j)] = value.astype(bf16)

            @pl.when(jnp.logical_not(tip))
            def _():
                self.to_outer(i, t, k).wait_recv()
                for j, value in enumerate(own):
                    self.part[i, k, :, self.columns(j)] = (
                        value + self.outer[i, k, :, self.columns(j)].astype(f32)
                    ).astype(bf16)

            @pl.when(middle)
            def _():
                self.to_partner(i, t, k).start()

            @pl.when(jnp.logical_not(middle))
            def _():
                self.to_outer(i, t, k).start()

        def arrive(self, i, t, k):
            @pl.when(jnp.logical_not(middle))
            def _():
                self.to_partner(i, t, k).wait_recv()

            @pl.when(jnp.logical_not(jnp.logical_or(middle, tip)))
            def _():
                self.pass_out(i, t, k).start()

        def total(self, i, k, j):
            mine = self.part[i, k, :, self.columns(j)].astype(f32)
            return self.inner[i, k, :, self.columns(j)].astype(f32) + jnp.where(
                middle, mine, jnp.zeros_like(mine)
            )

        def activate(self, i, c0, t):
            self.arrive(i, t, 0)
            self.arrive(i, t, 1)
            added = None
            for j in range(self.parts):
                c = c0 + j
                gate, up = self.total(i, 0, j), self.total(i, 1, j)
                logistic = 1.0 / (1.0 + jnp.exp(-gate))
                silu = gate * logistic
                product = silu * up
                self.slope[:, self.columns(j)] = up * logistic * (1.0 + gate * (1.0 - logistic))
                self.silu[:, self.columns(j)] = silu
                term = jnp.dot(product.astype(bf16), wd_v[c], preferred_element_type=f32)
                added = term if added is None else added + term
                cols = pl.ds(pl.multiple_of(c * width, width), width)
                if self.r0:
                    product = jnp.concatenate(
                        (jnp.zeros((self.r0, width), f32), product), axis=0
                    )
                hid_ref[cols, self.r0 : self.r1] = jnp.transpose(product)[:, self.r0 :].astype(bf16)
            out_acc[self.r0 : self.r1, :] += added

        def differentiate(self, i, c0, t):
            self.arrive(i, t, 2)
            added = None
            for j in range(self.parts):
                c = c0 + j
                down = self.total(i, 2, j)
                gate_grad = (down * self.slope[:, self.columns(j)]).astype(bf16)
                up_grad = (down * self.silu[:, self.columns(j)]).astype(bf16)
                term = contract_cols(gate_grad, wg_v[c]) + contract_cols(up_grad, wu_v[c])
                added = term if added is None else added + term
                cols = pl.ds(pl.multiple_of(c * width, width), width)
                gg_ref[self.r0 : self.r1, cols] = gate_grad
                ug_ref[self.r0 : self.r1, cols] = up_grad
            back_acc[self.r0 : self.r1, :] += added

        def drain(self, i, t):
            for k in range(3):
                self.to_outer(i, t, k).wait_send()

                @pl.when(jnp.logical_not(tip))
                def _():
                    self.sum_out(i, t, k).wait_send()

    tall = Kind(part_t, outer_t, inner_t, full_t, slope_t, silu_t, near, rows, 1)
    wide = Kind(part_w, outer_w, inner_w, full_w, slope_w, silu_w, 0, near, span)
    whole = Kind(part_f, outer_f, inner_f, full_f, slope_f, silu_f, 0, rows, 1)

    def return_copy(which, slot):
        to = device_of(slot)
        return pltpu.make_async_remote_copy(
            src_ref=y_send.at[which, slot], dst_ref=y_recv.at[which, me],
            send_sem=ys_sem.at[which, slot],
            recv_sem=yr_sem.at[which, me],
            device_id={"dp": to}, device_id_type=MESH,
        )

    def return_take(which, slot):
        source = device_of(slot)
        pltpu.make_async_remote_copy(
            src_ref=y_send.at[which, slot], dst_ref=y_recv.at[which, source],
            send_sem=ys_sem.at[which, slot],
            recv_sem=yr_sem.at[which, source],
            device_id={"dp": source}, device_id_type=MESH,
        ).wait()

    def home_far(which, acc):
        y_send[which, CORES:] = acc[near:, :].astype(bf16).reshape(groups - CORES, cap, feats)

        @pl.loop(CORES, groups)
        def _(slot):
            return_copy(which, slot).start()

    def home_near(which, acc):
        y_send[which, :CORES] = acc[:near, :].astype(bf16).reshape(CORES, cap, feats)
        return_copy(which, 1 - core).start()
        y_recv[which, me] = y_send[which, core]

    lag = jnp.where(middle, 2, 2 + 4 * distance)
    last = units - 1

    def each_kind(t, body):
        @pl.when(jnp.logical_or(t == 0, t == last))
        def _():
            body(wide, jnp.where(t == 0, 0, 1), jnp.where(t == 0, 0, chunks - span), t)

        c = t - 1
        edge = jnp.logical_or(c < span, c >= chunks - span)
        inside = jnp.logical_and(c >= 0, c < chunks)

        @pl.when(jnp.logical_and(inside, edge))
        def _():
            body(tall, jnp.where(c < span, c, c - (chunks - 2 * span)), c, t)

        @pl.when(jnp.logical_and(inside, jnp.logical_not(edge)))
        def _():
            body(whole, c - span, c, t)

    def wait_weights(c0, parts, k):
        for j in range(parts):
            weight_copy(c0 + j, k).wait()

    @pl.loop(0, units + 2 + 4 * (half - 1))
    def _(t):
        before, done = t - 1, t - lag
        for k in range(3):

            def start(kind, i, c0, t):
                if kind is wide:

                    @pl.when(t == 0)
                    def _():
                        wait_weights(0, span, k)
                        if k == 0:
                            row_take(tok_ref, x_v, 0, 1 - core)
                        if k == 2:
                            row_take(grd_ref, g_v, 1, 1 - core)

                else:

                    @pl.when(c0 >= span)
                    def _():
                        wait_weights(c0, 1, k)

                if kind is tall and k != 1:

                    @pl.when(c0 == 0)
                    def _():
                        if k == 0:
                            take_far(0, tok_ref, x_v)
                        else:
                            take_far(1, grd_ref, g_v)

                kind.gather(i, c0, t, k)

            each_kind(t, start)

            @pl.when(middle)
            def _():
                each_kind(before, lambda kind, i, c0, t: kind.forward(i, t, k))

            if k == 0:
                each_kind(done, lambda kind, i, c0, t: kind.activate(i, c0, t))

                @pl.when(done == last - 1)
                def _():
                    home_far(0, out_acc)

                @pl.when(done == last)
                def _():
                    home_near(0, out_acc)

            if k == 1:
                each_kind(done, lambda kind, i, c0, t: kind.differentiate(i, c0, t))

                @pl.when(done == last - 1)
                def _():
                    home_far(1, back_acc)

                @pl.when(done == last)
                def _():
                    home_near(1, back_acc)

        @pl.when(t == 2)
        def _():
            xt_ref[...] = jnp.transpose(x_v[...].astype(f32)).astype(bf16)
            g_ref[...] = g_v[...]

        per = broad // width
        for which, source in enumerate((gg_ref, ug_ref)):
            ready = done - which
            block = ready // per - 1

            @pl.when(
                jnp.logical_and(
                    jnp.logical_and(ready >= per, block < early), lax.rem(ready, per) == 0
                )
            )
            def _():
                cols = pl.ds(pl.multiple_of(block * broad, broad), broad)
                soon_ref[which, block] = jnp.dot(
                    xt_ref[...], source[:, cols], preferred_element_type=f32
                ).astype(bf16)

    @pl.loop(0, units)
    def _(t):
        each_kind(t, lambda kind, i, c0, t: kind.drain(i, t))

    for which in range(2):
        row_copy(tok_ref, x_v, which, 1 - core).wait_send()
        return_take(which, 1 - core)

        @pl.loop(CORES, groups)
        def _(slot):
            row_copy(tok_ref, x_v, which, slot).wait_send()
            return_take(which, slot)

    back_ref[...] = y_recv[...]


def run_window(ids, gates, tokens, cotangent, w_gate, w_up, w_down):
    groups, size = lax.axis_size("dp"), lax.axis_size("eshard")
    members = groups // EXPERTS
    feats, hidden = w_gate.shape
    cap, count = CAP, tokens.shape[0]
    rows, near = groups * cap, CORES * cap
    width = min(WIDTH, hidden)
    chunks = hidden // width
    span = max(1, min(SPAN, chunks // 4))
    units = chunks + 2
    broad = min(GRAD_WIDTH, hidden)
    early = max(1, min(EARLY, (chunks - span) // (2 * (broad // width))))
    bf16, f32 = jnp.bfloat16, jnp.float32
    vmem, hbm = pl.BlockSpec(memory_space=pltpu.VMEM), pl.BlockSpec(memory_space=pl.ANY)
    dma = pltpu.SemaphoreType.DMA
    gathered = jax.ShapeDtypeStruct((rows, hidden), bf16)
    tall = pltpu.VMEM((2 * span, 3, rows - near, width), bf16)
    wide = pltpu.VMEM((2, 3, near, span * width), bf16)
    whole = pltpu.VMEM((chunks - 2 * span, 3, rows, width), bf16)
    tall_f32 = pltpu.VMEM((rows - near, width), f32)
    wide_f32 = pltpu.VMEM((near, span * width), f32)
    whole_f32 = pltpu.VMEM((rows, width), f32)
    return pl.pallas_call(
        functools.partial(window_kernel, size, groups, members, chunks, width, cap, span, early, broad),
        out_shape=(
            jax.ShapeDtypeStruct((hidden, rows), bf16), gathered, gathered,
            jax.ShapeDtypeStruct((feats, rows), bf16),
            jax.ShapeDtypeStruct((rows, feats), bf16),
            jax.ShapeDtypeStruct((2, groups, cap, feats), bf16),
            jax.ShapeDtypeStruct((3, count, EXPERTS * cap), bf16),
            jax.ShapeDtypeStruct((2, early, feats, broad), bf16),
        ),
        in_specs=[hbm] * 7,
        out_specs=(vmem,) * 8,
        scratch_shapes=[
            pltpu.VMEM(ids.shape, jnp.int32),
            pltpu.VMEM(gates.shape, jnp.int32),
            pltpu.VMEM(tokens.shape, bf16),
            pltpu.VMEM(cotangent.shape, bf16),
            pltpu.VMEM((EXPERTS * cap, feats), bf16),
            pltpu.VMEM((EXPERTS * cap, feats), bf16),
            pltpu.VMEM((chunks, feats, width), bf16),
            pltpu.VMEM((chunks, feats, width), bf16),
            pltpu.VMEM((chunks, width, feats), bf16),
            pltpu.VMEM((rows, feats), bf16),
            pltpu.VMEM((rows, feats), bf16),
            tall, tall, tall, tall, tall_f32, tall_f32,
            wide, wide, wide, wide, wide_f32, wide_f32,
            whole, whole, whole, whole, whole_f32, whole_f32,
            pltpu.VMEM((rows, feats), f32),
            pltpu.VMEM((rows, feats), f32),
            pltpu.VMEM((2, groups, cap, feats), bf16),
            pltpu.VMEM((2, groups, cap, feats), bf16),
            dma((4,)), dma((chunks, 3)),
            dma((2, groups)), dma((2, groups)),
            dma((units, 3)), dma((units, 3)), dma((units, 3)), dma((units, 3)),
            dma((2, groups)), dma((2, groups)),
        ],
        compiler_params=pltpu.CompilerParams(
            collective_id=0, has_side_effects=True, vmem_limit_bytes=VMEM_BYTES
        ),
    )(ids, gates, tokens, cotangent, w_gate, w_up, w_down)


def gradient_kernel(
    members, width, xt_ref, gg_ref, ug_ref, hid_ref, g_ref, back_ref, pick_ref, soon_ref,
    mixed_ref, token_ref, gate_ref, up_ref, down_ref,
    mixed_v, token_v, gate_v, up_v, down_v, row_sem, sem,
):
    f32, bf16 = jnp.float32, jnp.bfloat16

    def product(left, right):
        return jnp.dot(left, right, preferred_element_type=f32)

    early = soon_ref.shape[1]
    blocks = down_v.shape[0]

    def columns(i):
        return pl.ds(pl.multiple_of(i * width, width), width)

    def soon_copy(which, i):
        target = gate_ref if which == 0 else up_ref
        return pltpu.make_async_copy(
            soon_ref.at[which, i], target.at[:, columns(i)], sem.at[i, which]
        )

    def gate_copy(i):
        return pltpu.make_async_copy(gate_v.at[i - early], gate_ref.at[:, columns(i)], sem.at[i, 0])

    def up_copy(i):
        return pltpu.make_async_copy(up_v.at[i - early], up_ref.at[:, columns(i)], sem.at[i, 1])

    def down_copy(i):
        return pltpu.make_async_copy(down_v.at[i], down_ref.at[columns(i), :], sem.at[i, 2])

    def make_down(i):
        down_v[i] = product(hid_ref[columns(i), :], g_ref[...]).astype(bf16)
        down_copy(i).start()

    @pl.loop(0, early)
    def _(i):
        for which in range(2):
            soon_copy(which, i).start()

    @pl.loop(0, early)
    def _(i):
        make_down(i)

    @pl.loop(early, blocks)
    def _(i):
        gate_v[i - early] = product(xt_ref[...], gg_ref[:, columns(i)]).astype(bf16)
        gate_copy(i).start()
        up_v[i - early] = product(xt_ref[...], ug_ref[:, columns(i)]).astype(bf16)
        up_copy(i).start()
        make_down(i)

    def gathered(which):
        parts = []
        for expert in range(EXPERTS):
            total = back_ref[which, expert * members].astype(f32)
            for member in range(1, members):
                total = total + back_ref[which, expert * members + member].astype(f32)
            parts.append(total)
        return halves(jnp.concatenate(parts, axis=0))

    high, low = gathered(0)
    mixed_v[...] = (
        product(pick_ref[1], high) + product(pick_ref[2], high) + product(pick_ref[1], low)
    ).astype(bf16)
    mixed_copy = pltpu.make_async_copy(mixed_v, mixed_ref, row_sem.at[0])
    mixed_copy.start()
    high, low = gathered(1)
    token_v[...] = (product(pick_ref[0], high) + product(pick_ref[0], low)).astype(bf16)
    token_copy = pltpu.make_async_copy(token_v, token_ref, row_sem.at[1])
    token_copy.start()

    @pl.loop(0, early)
    def _(i):
        for which in range(2):
            soon_copy(which, i).wait()
        down_copy(i).wait()

    @pl.loop(early, blocks)
    def _(i):
        gate_copy(i).wait()
        up_copy(i).wait()
        down_copy(i).wait()

    mixed_copy.wait()
    token_copy.wait()


def run_gradients(count, hidden_t, gate_grad, up_grad, inputs_t, route_grad, back, pick, soon):
    groups = lax.axis_size("dp")
    feats = inputs_t.shape[0]
    hidden = hidden_t.shape[0]
    width = min(GRAD_WIDTH, hidden)
    blocks = hidden // width
    bf16 = jnp.bfloat16
    vmem, hbm = pl.BlockSpec(memory_space=pltpu.VMEM), pl.BlockSpec(memory_space=pl.ANY)
    return pl.pallas_call(
        functools.partial(gradient_kernel, groups // EXPERTS, width),
        out_shape=(
            jax.ShapeDtypeStruct((count, feats), bf16),
            jax.ShapeDtypeStruct((count, feats), bf16),
            jax.ShapeDtypeStruct((feats, hidden), bf16),
            jax.ShapeDtypeStruct((feats, hidden), bf16),
            jax.ShapeDtypeStruct((hidden, feats), bf16),
        ),
        in_specs=[vmem] * 8,
        out_specs=(hbm,) * 5,
        scratch_shapes=[
            pltpu.VMEM((count, feats), bf16),
            pltpu.VMEM((count, feats), bf16),
            pltpu.VMEM((blocks - soon.shape[1], feats, width), bf16),
            pltpu.VMEM((blocks - soon.shape[1], feats, width), bf16),
            pltpu.VMEM((blocks, width, feats), bf16),
            pltpu.SemaphoreType.DMA((2,)),
            pltpu.SemaphoreType.DMA((blocks, 3)),
        ],
        compiler_params=pltpu.CompilerParams(vmem_limit_bytes=GRAD_BYTES),
    )(inputs_t, gate_grad, up_grad, hidden_t, route_grad, back, pick, soon)


def on_device(tokens, cotangent, route_ids, gate_fixed, w_gate, w_up, w_down):
    hidden_t, gate_grad, up_grad, inputs_t, route_grad, back, pick, soon = run_window(
        *(pltpu.with_memory_space_constraint(a, pltpu.HBM) for a in (jnp.transpose(route_ids), jnp.transpose(gate_fixed), tokens, cotangent)), w_gate, w_up, w_down
    )
    return run_gradients(
        tokens.shape[0], hidden_t, gate_grad, up_grad, inputs_t, route_grad, back, pick, soon
    )


def solution(mesh):
    placed = (
        P("dp", "eshard"),
        P("dp", "eshard"),
        P("dp", None),
        P("dp", None),
        P("eshard", "dp"),
        P("eshard", "dp"),
        P("dp", "eshard"),
    )
    return jax.shard_map(
        on_device,
        mesh=mesh,
        in_specs=placed,
        out_specs=(
            P("dp", "eshard"),
            P("dp", "eshard"),
            P("eshard", "dp"),
            P("eshard", "dp"),
            P("dp", "eshard"),
        ),
        check_vma=False,
    )
```

```python
import functools

import jax
import jax.numpy as jnp
from jax import lax
from jax.experimental import pallas as pl
from jax.experimental.pallas import tpu as pltpu
from jax.sharding import PartitionSpec as P

EXPERTS = 4
CAP = 16
CORES = 2
WIDTH = 256
SPAN = 4
GRAD_WIDTH = 512
EARLY = 4
VMEM_BYTES = 43 * 1024 * 1024
GRAD_BYTES = 27 * 1024 * 1024


MESH = pl.DeviceIdType.MESH


def contract_cols(left, right):
    return lax.dot_general(
        left, right, (((1,), (1,)), ((), ())), preferred_element_type=jnp.float32
    )


def halves(value):
    high = value.astype(jnp.bfloat16)
    return high, (value - high.astype(jnp.float32)).astype(jnp.bfloat16)


def routing(ids, gates, cap):
    tokens = ids.shape[1]
    f32 = jnp.float32
    values = gates.astype(f32) * (1.0 / 65536.0)
    hits, weights = [], []
    for expert in range(EXPERTS):
        named = (ids == expert).astype(f32)
        hits.append(jnp.sum(named, axis=0, keepdims=True))
        weights.append(jnp.sum(named * values, axis=0, keepdims=True))
    hit = jnp.concatenate(hits, axis=0)
    earlier = (
        lax.broadcasted_iota(jnp.int32, (tokens, tokens), 0)
        < lax.broadcasted_iota(jnp.int32, (tokens, tokens), 1)
    ).astype(jnp.bfloat16)
    slots = jnp.dot(hit.astype(jnp.bfloat16), earlier, preferred_element_type=f32)
    places = lax.broadcasted_iota(jnp.int32, (cap, tokens), 0).astype(f32)
    select, weighted = [], []
    for expert in range(EXPERTS):
        here = (places == slots[expert : expert + 1]).astype(f32) * hits[expert]
        select.append(here)
        weighted.append(here * weights[expert])
    return jnp.concatenate(select, axis=0), jnp.concatenate(weighted, axis=0)


def window_kernel(
    size, groups, members, chunks, width, cap, span, early, broad,
    ids_ref, gates_ref, tokens_ref, cot_ref, wg_ref, wu_ref, wd_ref,
    hid_ref, gg_ref, ug_ref, xt_ref, g_ref, back_ref, pick_ref, soon_ref,
    ids_v, gates_v, tokens_v, cot_v, tok_ref, grd_ref, wg_v, wu_v, wd_v, x_v, g_v,
    part_t, outer_t, inner_t, full_t, slope_t, silu_t,
    part_w, outer_w, inner_w, full_w, slope_w, silu_w,
    part_f, outer_f, inner_f, full_f, slope_f, silu_f,
    out_acc, back_acc, y_send, y_recv,
    a_sem, w_sem, xs_sem, xr_sem, in_sem, outer_sem, inner_sem, out_sem, ys_sem, yr_sem,
):
    f32, bf16 = jnp.float32, jnp.bfloat16
    me, z = lax.axis_index("dp"), lax.axis_index("eshard")
    chips = groups // CORES
    chip, core = me // CORES, lax.rem(me, CORES)
    feats = tok_ref.shape[1]
    near = CORES * cap
    rows = groups * cap
    units = chunks + 2
    half = size // 2
    left = z < half
    middle = jnp.logical_or(z == half - 1, z == half)
    tip = jnp.logical_or(z == 0, z == size - 1)
    inward = jnp.where(left, z + 1, z - 1)
    outward = jnp.where(tip, z, jnp.where(left, z - 1, z + 1))
    distance = jnp.where(left, half - 1 - z, z - half)

    small = tuple(
        pltpu.make_async_copy(src, dst, a_sem.at[i])
        for i, (src, dst) in enumerate(
            ((ids_ref, ids_v), (gates_ref, gates_v), (tokens_ref, tokens_v), (cot_ref, cot_v))
        )
    )
    for copy in small:
        copy.start()

    def weight_copy(c, k):
        cols = pl.ds(pl.multiple_of(c * width, width), width)
        if k == 0:
            return pltpu.make_async_copy(wg_ref.at[:, cols], wg_v.at[c], w_sem.at[c, 0])
        if k == 1:
            return pltpu.make_async_copy(wu_ref.at[:, cols], wu_v.at[c], w_sem.at[c, 1])
        return pltpu.make_async_copy(wd_ref.at[cols, :], wd_v.at[c], w_sem.at[c, 2])

    for k in range(3):
        for c in range(span):
            weight_copy(c, k).start()

    barrier = pltpu.get_barrier_semaphore()

    @pl.loop(1, groups)
    def _(k):
        pl.semaphore_signal(
            barrier, inc=1, device_id={"dp": lax.rem(me + k, groups)}, device_id_type=MESH
        )

    pl.semaphore_signal(barrier, inc=1, device_id={"eshard": inward}, device_id_type=MESH)

    @pl.when(jnp.logical_not(tip))
    def _():
        pl.semaphore_signal(barrier, inc=1, device_id={"eshard": outward}, device_id_type=MESH)

    small[0].wait()
    small[1].wait()
    select, weighted = routing(ids_v[...], gates_v[...], cap)
    small[2].wait()
    tok_ref[...] = jnp.dot(
        select.astype(bf16), tokens_v[...], preferred_element_type=f32
    ).astype(bf16)

    pl.semaphore_wait(barrier, groups + jnp.where(tip, 0, 1))

    def device_of(slot):
        return lax.rem(chip + slot // CORES, chips) * CORES + lax.rem(slot, CORES)

    def row_copy(src, dst, which, slot):
        to = device_of(slot)
        there = lax.rem(chips - slot // CORES, chips) * CORES + core
        return pltpu.make_async_remote_copy(
            src_ref=src.at[pl.ds(pl.multiple_of((to // members) * cap, cap), cap), :],
            dst_ref=dst.at[pl.ds(pl.multiple_of(there * cap, cap), cap), :],
            send_sem=xs_sem.at[which, slot],
            recv_sem=xr_sem.at[which, there],
            device_id={"dp": to},
            device_id_type=MESH,
        )

    def row_take(src, dst, which, slot):
        pltpu.make_async_remote_copy(
            src_ref=src.at[pl.ds(0, cap), :],
            dst_ref=dst.at[pl.ds(pl.multiple_of(slot * cap, cap), cap), :],
            send_sem=xs_sem.at[which, slot],
            recv_sem=xr_sem.at[which, slot],
            device_id={"dp": device_of(slot)},
            device_id_type=MESH,
        ).wait_recv()

    def send_near(which, src, dst):
        row_copy(src, dst, which, 1 - core).start()
        own = pl.multiple_of((me // members) * cap, cap)
        dst[pl.ds(pl.multiple_of(core * cap, cap), cap), :] = src[pl.ds(own, cap), :]

    def send_far(which, src, dst):
        @pl.loop(CORES, groups)
        def _(slot):
            row_copy(src, dst, which, slot).start()

    def take_far(which, src, dst):
        @pl.loop(CORES, groups)
        def _(slot):
            row_take(src, dst, which, slot)

    send_near(0, tok_ref, x_v)
    high, low = halves(weighted)
    small[3].wait()
    grd_ref[...] = (
        jnp.dot(high, cot_v[...], preferred_element_type=f32)
        + jnp.dot(low, cot_v[...], preferred_element_type=f32)
    ).astype(bf16)
    send_near(1, grd_ref, g_v)
    send_far(0, tok_ref, x_v)
    send_far(1, grd_ref, g_v)

    pick_ref[0] = jnp.transpose(select).astype(bf16)
    high, low = halves(jnp.transpose(weighted))
    pick_ref[1] = high
    pick_ref[2] = low

    class Kind:
        def __init__(self, part, outer, inner, full, slope, silu, r0, r1, parts):
            self.part, self.outer, self.inner, self.full = part, outer, inner, full
            self.slope, self.silu = slope, silu
            self.r0, self.r1, self.parts = r0, r1, parts

        def send(self, src, dst, i, t, k, sent, got, to):
            return pltpu.make_async_remote_copy(
                src_ref=src.at[i, k], dst_ref=dst.at[i, k],
                send_sem=sent.at[t, k], recv_sem=got.at[t, k],
                device_id={"eshard": to}, device_id_type=MESH,
            )

        def to_outer(self, i, t, k):
            return self.send(self.part, self.outer, i, t, k, in_sem, outer_sem, inward)

        def to_partner(self, i, t, k):
            return self.send(self.part, self.inner, i, t, k, in_sem, inner_sem, inward)

        def sum_out(self, i, t, k):
            return self.send(self.full, self.inner, i, t, k, out_sem, inner_sem, outward)

        def pass_out(self, i, t, k):
            return self.send(self.inner, self.inner, i, t, k, out_sem, inner_sem, outward)

        def columns(self, j):
            return pl.ds(j * width, width)

        def forward(self, i, t, k):
            self.to_partner(i, t, k).wait_recv()
            self.full[i, k] = (
                self.part[i, k].astype(f32) + self.inner[i, k].astype(f32)
            ).astype(bf16)

            @pl.when(jnp.logical_not(tip))
            def _():
                self.sum_out(i, t, k).start()

        def gather(self, i, c0, t, k):
            own = []
            for j in range(self.parts):
                c = c0 + j
                if k == 0:
                    value = jnp.dot(x_v[self.r0 : self.r1, :], wg_v[c], preferred_element_type=f32)
                elif k == 1:
                    value = jnp.dot(x_v[self.r0 : self.r1, :], wu_v[c], preferred_element_type=f32)
                else:
                    value = contract_cols(g_v[self.r0 : self.r1, :], wd_v[c])
                own.append(value)

            @pl.when(tip)
            def _():
                for j, value in enumerate(own):
                    self.part[i, k, :, self.columns(j)] = value.astype(bf16)

            @pl.when(jnp.logical_not(tip))
            def _():
                self.to_outer(i, t, k).wait_recv()
                for j, value in enumerate(own):
                    self.part[i, k, :, self.columns(j)] = (
                        value + self.outer[i, k, :, self.columns(j)].astype(f32)
                    ).astype(bf16)

            @pl.when(middle)
            def _():
                self.to_partner(i, t, k).start()

            @pl.when(jnp.logical_not(middle))
            def _():
                self.to_outer(i, t, k).start()

        def arrive(self, i, t, k):
            @pl.when(jnp.logical_not(middle))
            def _():
                self.to_partner(i, t, k).wait_recv()

            @pl.when(jnp.logical_not(jnp.logical_or(middle, tip)))
            def _():
                self.pass_out(i, t, k).start()

        def total(self, i, k, j):
            mine = self.part[i, k, :, self.columns(j)].astype(f32)
            return self.inner[i, k, :, self.columns(j)].astype(f32) + jnp.where(
                middle, mine, jnp.zeros_like(mine)
            )

        def activate(self, i, c0, t):
            self.arrive(i, t, 0)
            self.arrive(i, t, 1)
            added = None
            for j in range(self.parts):
                c = c0 + j
                gate, up = self.total(i, 0, j), self.total(i, 1, j)
                logistic = 1.0 / (1.0 + jnp.exp(-gate))
                silu = gate * logistic
                product = silu * up
                self.slope[:, self.columns(j)] = up * logistic * (1.0 + gate * (1.0 - logistic))
                self.silu[:, self.columns(j)] = silu
                term = jnp.dot(product.astype(bf16), wd_v[c], preferred_element_type=f32)
                added = term if added is None else added + term
                cols = pl.ds(pl.multiple_of(c * width, width), width)
                if self.r0:
                    product = jnp.concatenate(
                        (jnp.zeros((self.r0, width), f32), product), axis=0
                    )
                hid_ref[cols, self.r0 : self.r1] = jnp.transpose(product)[:, self.r0 :].astype(bf16)
            out_acc[self.r0 : self.r1, :] += added

        def differentiate(self, i, c0, t):
            self.arrive(i, t, 2)
            added = None
            for j in range(self.parts):
                c = c0 + j
                down = self.total(i, 2, j)
                gate_grad = (down * self.slope[:, self.columns(j)]).astype(bf16)
                up_grad = (down * self.silu[:, self.columns(j)]).astype(bf16)
                term = contract_cols(gate_grad, wg_v[c]) + contract_cols(up_grad, wu_v[c])
                added = term if added is None else added + term
                cols = pl.ds(pl.multiple_of(c * width, width), width)
                gg_ref[self.r0 : self.r1, cols] = gate_grad
                ug_ref[self.r0 : self.r1, cols] = up_grad
            back_acc[self.r0 : self.r1, :] += added

        def drain(self, i, t):
            for k in range(3):
                self.to_outer(i, t, k).wait_send()

                @pl.when(jnp.logical_not(tip))
                def _():
                    self.sum_out(i, t, k).wait_send()

    tall = Kind(part_t, outer_t, inner_t, full_t, slope_t, silu_t, near, rows, 1)
    wide = Kind(part_w, outer_w, inner_w, full_w, slope_w, silu_w, 0, near, span)
    whole = Kind(part_f, outer_f, inner_f, full_f, slope_f, silu_f, 0, rows, 1)

    def return_copy(which, slot):
        to = device_of(slot)
        return pltpu.make_async_remote_copy(
            src_ref=y_send.at[which, slot], dst_ref=y_recv.at[which, me],
            send_sem=ys_sem.at[which, slot],
            recv_sem=yr_sem.at[which, me],
            device_id={"dp": to}, device_id_type=MESH,
        )

    def return_take(which, slot):
        source = device_of(slot)
        pltpu.make_async_remote_copy(
            src_ref=y_send.at[which, slot], dst_ref=y_recv.at[which, source],
            send_sem=ys_sem.at[which, slot],
            recv_sem=yr_sem.at[which, source],
            device_id={"dp": source}, device_id_type=MESH,
        ).wait()

    def home_far(which, acc):
        y_send[which, CORES:] = acc[near:, :].astype(bf16).reshape(groups - CORES, cap, feats)

        @pl.loop(CORES, groups)
        def _(slot):
            return_copy(which, slot).start()

    def home_near(which, acc):
        y_send[which, :CORES] = acc[:near, :].astype(bf16).reshape(CORES, cap, feats)
        return_copy(which, 1 - core).start()
        y_recv[which, me] = y_send[which, core]

    lag = jnp.where(middle, 2, 2 + 4 * distance)
    last = units - 1

    def each_kind(t, body):
        @pl.when(jnp.logical_or(t == 0, t == last))
        def _():
            body(wide, jnp.where(t == 0, 0, 1), jnp.where(t == 0, 0, chunks - span), t)

        c = t - 1
        edge = jnp.logical_or(c < span, c >= chunks - span)
        inside = jnp.logical_and(c >= 0, c < chunks)

        @pl.when(jnp.logical_and(inside, edge))
        def _():
            body(tall, jnp.where(c < span, c, c - (chunks - 2 * span)), c, t)

        @pl.when(jnp.logical_and(inside, jnp.logical_not(edge)))
        def _():
            body(whole, c - span, c, t)

    def wait_weights(c0, parts, k):
        for j in range(parts):
            weight_copy(c0 + j, k).wait()

    @pl.loop(0, units + 2 + 4 * (half - 1))
    def _(t):
        before, done = t - 1, t - lag
        for k in range(3):

            def start(kind, i, c0, t):
                if kind is wide:

                    @pl.when(t == 0)
                    def _():
                        wait_weights(0, span, k)
                        if k == 0:
                            row_take(tok_ref, x_v, 0, 1 - core)
                        if k == 2:
                            row_take(grd_ref, g_v, 1, 1 - core)

                else:

                    @pl.when(c0 >= span)
                    def _():
                        wait_weights(c0, 1, k)

                if kind is tall and k != 1:

                    @pl.when(c0 == 0)
                    def _():
                        if k == 0:
                            take_far(0, tok_ref, x_v)
                        else:
                            take_far(1, grd_ref, g_v)

                kind.gather(i, c0, t, k)

            each_kind(t, start)

            @pl.when(middle)
            def _():
                each_kind(before, lambda kind, i, c0, t: kind.forward(i, t, k))

            if k == 0:
                each_kind(done, lambda kind, i, c0, t: kind.activate(i, c0, t))

                @pl.when(done == last - 1)
                def _():
                    home_far(0, out_acc)

                @pl.when(done == last)
                def _():
                    home_near(0, out_acc)

            if k == 1:
                each_kind(done, lambda kind, i, c0, t: kind.differentiate(i, c0, t))

                @pl.when(done == last - 1)
                def _():
                    home_far(1, back_acc)

                @pl.when(done == last)
                def _():
                    home_near(1, back_acc)

        @pl.when(t == 0)
        def _():
            @pl.loop(span, chunks)
            def _(c):
                for k in range(3):
                    weight_copy(c, k).start()

            out_acc[...] = jnp.zeros_like(out_acc)
            back_acc[...] = jnp.zeros_like(back_acc)

        @pl.when(t == 2)
        def _():
            xt_ref[...] = jnp.transpose(x_v[...].astype(f32)).astype(bf16)
            g_ref[...] = g_v[...]

        per = broad // width
        for which, source in enumerate((gg_ref, ug_ref)):
            ready = done - which
            block = ready // per - 1

            @pl.when(
                jnp.logical_and(
                    jnp.logical_and(ready >= per, block < early), lax.rem(ready, per) == 0
                )
            )
            def _():
                cols = pl.ds(pl.multiple_of(block * broad, broad), broad)
                soon_ref[which, block] = jnp.dot(
                    xt_ref[...], source[:, cols], preferred_element_type=f32
                ).astype(bf16)

    @pl.loop(0, units)
    def _(t):
        each_kind(t, lambda kind, i, c0, t: kind.drain(i, t))

    for which in range(2):
        row_copy(tok_ref, x_v, which, 1 - core).wait_send()
        return_take(which, 1 - core)

        @pl.loop(CORES, groups)
        def _(slot):
            row_copy(tok_ref, x_v, which, slot).wait_send()
            return_take(which, slot)

    back_ref[...] = y_recv[...]


def run_window(ids, gates, tokens, cotangent, w_gate, w_up, w_down):
    groups, size = lax.axis_size("dp"), lax.axis_size("eshard")
    members = groups // EXPERTS
    feats, hidden = w_gate.shape
    cap, count = CAP, tokens.shape[0]
    rows, near = groups * cap, CORES * cap
    width = min(WIDTH, hidden)
    chunks = hidden // width
    span = max(1, min(SPAN, chunks // 4))
    units = chunks + 2
    broad = min(GRAD_WIDTH, hidden)
    early = max(1, min(EARLY, (chunks - span) // (2 * (broad // width))))
    bf16, f32 = jnp.bfloat16, jnp.float32
    vmem, hbm = pl.BlockSpec(memory_space=pltpu.VMEM), pl.BlockSpec(memory_space=pl.ANY)
    dma = pltpu.SemaphoreType.DMA
    gathered = jax.ShapeDtypeStruct((rows, hidden), bf16)
    tall = pltpu.VMEM((2 * span, 3, rows - near, width), bf16)
    wide = pltpu.VMEM((2, 3, near, span * width), bf16)
    whole = pltpu.VMEM((chunks - 2 * span, 3, rows, width), bf16)
    tall_f32 = pltpu.VMEM((rows - near, width), f32)
    wide_f32 = pltpu.VMEM((near, span * width), f32)
    whole_f32 = pltpu.VMEM((rows, width), f32)
    return pl.pallas_call(
        functools.partial(window_kernel, size, groups, members, chunks, width, cap, span, early, broad),
        out_shape=(
            jax.ShapeDtypeStruct((hidden, rows), bf16), gathered, gathered,
            jax.ShapeDtypeStruct((feats, rows), bf16),
            jax.ShapeDtypeStruct((rows, feats), bf16),
            jax.ShapeDtypeStruct((2, groups, cap, feats), bf16),
            jax.ShapeDtypeStruct((3, count, EXPERTS * cap), bf16),
            jax.ShapeDtypeStruct((2, early, feats, broad), bf16),
        ),
        in_specs=[hbm] * 7,
        out_specs=(vmem,) * 8,
        scratch_shapes=[
            pltpu.VMEM(ids.shape, jnp.int32),
            pltpu.VMEM(gates.shape, jnp.int32),
            pltpu.VMEM(tokens.shape, bf16),
            pltpu.VMEM(cotangent.shape, bf16),
            pltpu.VMEM((EXPERTS * cap, feats), bf16),
            pltpu.VMEM((EXPERTS * cap, feats), bf16),
            pltpu.VMEM((chunks, feats, width), bf16),
            pltpu.VMEM((chunks, feats, width), bf16),
            pltpu.VMEM((chunks, width, feats), bf16),
            pltpu.VMEM((rows, feats), bf16),
            pltpu.VMEM((rows, feats), bf16),
            tall, tall, tall, tall, tall_f32, tall_f32,
            wide, wide, wide, wide, wide_f32, wide_f32,
            whole, whole, whole, whole, whole_f32, whole_f32,
            pltpu.VMEM((rows, feats), f32),
            pltpu.VMEM((rows, feats), f32),
            pltpu.VMEM((2, groups, cap, feats), bf16),
            pltpu.VMEM((2, groups, cap, feats), bf16),
            dma((4,)), dma((chunks, 3)),
            dma((2, groups)), dma((2, groups)),
            dma((units, 3)), dma((units, 3)), dma((units, 3)), dma((units, 3)),
            dma((2, groups)), dma((2, groups)),
        ],
        compiler_params=pltpu.CompilerParams(
            collective_id=0, has_side_effects=True, vmem_limit_bytes=VMEM_BYTES
        ),
    )(ids, gates, tokens, cotangent, w_gate, w_up, w_down)


def gradient_kernel(
    members, width, xt_ref, gg_ref, ug_ref, hid_ref, g_ref, back_ref, pick_ref, soon_ref,
    mixed_ref, token_ref, gate_ref, up_ref, down_ref,
    mixed_v, token_v, gate_v, up_v, down_v, row_sem, sem,
):
    f32, bf16 = jnp.float32, jnp.bfloat16

    def product(left, right):
        return jnp.dot(left, right, preferred_element_type=f32)

    early = soon_ref.shape[1]
    blocks = down_v.shape[0]

    def columns(i):
        return pl.ds(pl.multiple_of(i * width, width), width)

    def soon_copy(which, i):
        target = gate_ref if which == 0 else up_ref
        return pltpu.make_async_copy(
            soon_ref.at[which, i], target.at[:, columns(i)], sem.at[i, which]
        )

    def gate_copy(i):
        return pltpu.make_async_copy(gate_v.at[i - early], gate_ref.at[:, columns(i)], sem.at[i, 0])

    def up_copy(i):
        return pltpu.make_async_copy(up_v.at[i - early], up_ref.at[:, columns(i)], sem.at[i, 1])

    def down_copy(i):
        return pltpu.make_async_copy(down_v.at[i], down_ref.at[columns(i), :], sem.at[i, 2])

    def make_down(i):
        down_v[i] = product(hid_ref[columns(i), :], g_ref[...]).astype(bf16)
        down_copy(i).start()

    @pl.loop(0, early)
    def _(i):
        for which in range(2):
            soon_copy(which, i).start()

    @pl.loop(0, early)
    def _(i):
        make_down(i)

    @pl.loop(early, blocks)
    def _(i):
        gate_v[i - early] = product(xt_ref[...], gg_ref[:, columns(i)]).astype(bf16)
        gate_copy(i).start()
        up_v[i - early] = product(xt_ref[...], ug_ref[:, columns(i)]).astype(bf16)
        up_copy(i).start()
        make_down(i)

    def gathered(which):
        parts = []
        for expert in range(EXPERTS):
            total = back_ref[which, expert * members].astype(f32)
            for member in range(1, members):
                total = total + back_ref[which, expert * members + member].astype(f32)
            parts.append(total)
        return halves(jnp.concatenate(parts, axis=0))

    high, low = gathered(0)
    mixed_v[...] = (
        product(pick_ref[1], high) + product(pick_ref[2], high) + product(pick_ref[1], low)
    ).astype(bf16)
    mixed_copy = pltpu.make_async_copy(mixed_v, mixed_ref, row_sem.at[0])
    mixed_copy.start()
    high, low = gathered(1)
    token_v[...] = (product(pick_ref[0], high) + product(pick_ref[0], low)).astype(bf16)
    token_copy = pltpu.make_async_copy(token_v, token_ref, row_sem.at[1])
    token_copy.start()

    @pl.loop(0, early)
    def _(i):
        for which in range(2):
            soon_copy(which, i).wait()
        down_copy(i).wait()

    @pl.loop(early, blocks)
    def _(i):
        gate_copy(i).wait()
        up_copy(i).wait()
        down_copy(i).wait()

    mixed_copy.wait()
    token_copy.wait()


def run_gradients(count, hidden_t, gate_grad, up_grad, inputs_t, route_grad, back, pick, soon):
    groups = lax.axis_size("dp")
    feats = inputs_t.shape[0]
    hidden = hidden_t.shape[0]
    width = min(GRAD_WIDTH, hidden)
    blocks = hidden // width
    bf16 = jnp.bfloat16
    vmem, hbm = pl.BlockSpec(memory_space=pltpu.VMEM), pl.BlockSpec(memory_space=pl.ANY)
    return pl.pallas_call(
        functools.partial(gradient_kernel, groups // EXPERTS, width),
        out_shape=(
            jax.ShapeDtypeStruct((count, feats), bf16),
            jax.ShapeDtypeStruct((count, feats), bf16),
            jax.ShapeDtypeStruct((feats, hidden), bf16),
            jax.ShapeDtypeStruct((feats, hidden), bf16),
            jax.ShapeDtypeStruct((hidden, feats), bf16),
        ),
        in_specs=[vmem] * 8,
        out_specs=(hbm,) * 5,
        scratch_shapes=[
            pltpu.VMEM((count, feats), bf16),
            pltpu.VMEM((count, feats), bf16),
            pltpu.VMEM((blocks - soon.shape[1], feats, width), bf16),
            pltpu.VMEM((blocks - soon.shape[1], feats, width), bf16),
            pltpu.VMEM((blocks, width, feats), bf16),
            pltpu.SemaphoreType.DMA((2,)),
            pltpu.SemaphoreType.DMA((blocks, 3)),
        ],
        compiler_params=pltpu.CompilerParams(vmem_limit_bytes=GRAD_BYTES),
    )(inputs_t, gate_grad, up_grad, hidden_t, route_grad, back, pick, soon)


def on_device(tokens, cotangent, route_ids, gate_fixed, w_gate, w_up, w_down):
    hidden_t, gate_grad, up_grad, inputs_t, route_grad, back, pick, soon = run_window(
        *(pltpu.with_memory_space_constraint(a, pltpu.HBM) for a in (jnp.transpose(route_ids), jnp.transpose(gate_fixed), tokens, cotangent)), w_gate, w_up, w_down
    )
    return run_gradients(
        tokens.shape[0], hidden_t, gate_grad, up_grad, inputs_t, route_grad, back, pick, soon
    )


def solution(mesh):
    placed = (
        P("dp", "eshard"),
        P("dp", "eshard"),
        P("dp", None),
        P("dp", None),
        P("eshard", "dp"),
        P("eshard", "dp"),
        P("dp", "eshard"),
    )
    return jax.shard_map(
        on_device,
        mesh=mesh,
        in_specs=placed,
        out_specs=(
            P("dp", "eshard"),
            P("dp", "eshard"),
            P("eshard", "dp"),
            P("eshard", "dp"),
            P("dp", "eshard"),
        ),
        check_vma=False,
    )
```
